32 devices in a mesh: row: 8 (over z, y), feat: 4 (over x, core).
Axes of the slice: x: 2, y: 2, z: 4, core: 2. Of those that a mesh axis runs over, the one named last changes fastest.
Arguments:
- design: bfloat16 [1024, 65536], P('row', 'feat'), may hold values from -0.0234375 to 0.0234375
- targets: bfloat16 [1024, 48], P('row'), may hold values from -6 to 6
- factor: float32 [65536, 256], P(('feat', 'row')), may hold values from -0.09375 to 0.09375
- weights: float32 [256], replicated, may hold values from 0.3 to 3
- penalty: float32 [48], replicated, may hold values from 0.05 to 0.5
Outputs:
- solution: float32 [65536, 48], P(('feat', 'row'))
- residual: float32 [65536, 48], P(('feat', 'row'))
The draws below stay inside these ranges and needn't reach their ends.
All inputs are finite; a program needn't handle non-finite values.
Results may differ from the reference program's by a relative error of at most 0.024.
Values may be sent and summed in bfloat16 or wider, within the bound.
A program may use at most 64 MiB of HBM per device.

```python
import math
import jax
import jax.numpy as jnp
from jax import lax

FEATURES = 65536
RANK = 256
TARGETS = 48
ROW_DEV = 128
ITERS = 3
ROWS = 1024
N_ROW = 8


def shard_levels(own_key, shape, shards, least, high):
    gain = 1.0
    for axis_at, blocks in shards:
        heights = jax.random.uniform(jax.random.fold_in(jax.random.fold_in(own_key, 6), axis_at), (blocks,), jnp.float32, least / len(shards), high / len(shards))
        gain = gain * jnp.repeat(jnp.exp(heights), shape[axis_at] // blocks).reshape((-1,) + (1,) * (len(shape) - 1 - axis_at))
    return gain


def centred(rng, extent, deviation, reach, cuts=(), held_as=jnp.bfloat16):
    gain = shard_levels(rng, extent, cuts, -0.22, 0.18) if cuts else 1.0
    entries = jax.random.normal(rng, extent, jnp.float32) * deviation * gain
    return jnp.minimum(jnp.maximum(entries, -reach), reach).astype(held_as)


def setup_inputs(seed: int = 0) -> dict:
    streams_of = jax.random.split(jax.random.key(seed), 6)
    return {
        "design": centred(streams_of[0], (ROWS, FEATURES), FEATURES ** -0.5, 0.0234375, ((0, 8), (1, 4))),
        "targets": centred(streams_of[1], (ROWS, TARGETS), 1.0, 6.0, ((0, 8),)),
        "factor": centred(streams_of[2], (FEATURES, RANK), (16 * RANK) ** -0.5, 0.09375, ((0, 32),), jnp.float32),
        "weights": jnp.clip(jnp.exp(jax.random.uniform(streams_of[3], (RANK,), jnp.float32, math.log(0.3), math.log(3.0))), 0.3, 3.0),
        "penalty": jnp.clip(jnp.exp(jax.random.uniform(streams_of[4], (TARGETS,), jnp.float32, math.log(0.05), math.log(0.5))), 0.05, 0.5),
    }


def row_blocks(design):
    return design.reshape(N_ROW, ROW_DEV, FEATURES)


def times_vector(design, vector_low):
    parts = lax.map(lambda segment: jnp.dot(segment, vector_low, preferred_element_type=jnp.float32), row_blocks(design))
    return parts.reshape(ROW_DEV * N_ROW, vector_low.shape[1])


def transpose_times(design, rows_low):
    blocks = row_blocks(design)
    pieces = rows_low.reshape(N_ROW, ROW_DEV, rows_low.shape[1])

    def accumulate(running, items):
        segment, values = items
        return running + lax.dot_general(segment, values, (((0,), (0,)), ((), ())), preferred_element_type=jnp.float32), None

    running = jnp.zeros((FEATURES, rows_low.shape[1]), jnp.float32)
    running, unused = lax.scan(accumulate, running, (blocks, pieces))
    return running


def precondition(factor, weights, vector):
    projected = jnp.dot(factor.T, vector, precision=lax.Precision.HIGHEST)
    return vector + jnp.dot(factor, weights[:, None] * projected, precision=lax.Precision.HIGHEST)


def reference(design, targets, factor, weights, penalty):
    residual = transpose_times(design, targets)
    solution = jnp.zeros_like(residual)
    search = precondition(factor, weights, residual)
    inner = jnp.sum(residual * search, axis=0)
    direction = search
    for step_index in range(ITERS):
        dir_low = direction.astype(jnp.bfloat16)
        row_values = times_vector(design, dir_low)
        row_low = row_values.astype(jnp.bfloat16)
        hessian_dir = transpose_times(design, row_low) + penalty[None, :] * direction
        curvature = jnp.sum(direction * hessian_dir, axis=0)
        step_size = inner / curvature
        solution = solution + step_size[None, :] * direction
        residual = residual - step_size[None, :] * hessian_dir
        if step_index + 1 < ITERS:
            search = precondition(factor, weights, residual)
            inner_next = jnp.sum(residual * search, axis=0)
            direction = search + (inner_next / inner)[None, :] * direction
            inner = inner_next
    return solution, residual
```

```python
import functools

import jax
import jax.numpy as jnp
from jax import lax
from jax.experimental import pallas as pl
from jax.experimental.pallas import tpu as pltpu
from jax.sharding import PartitionSpec as P

ITERS = 3
EXTRA = 16
LANES = 128
F32 = jnp.float32
BF16 = jnp.bfloat16
NT = (((1,), (1,)), ((), ()))


def to_column(row, count):
    return jnp.broadcast_to(row, (LANES, LANES)).T[:count, :1]


def kernel(
    n_row, n_feat, tile,
    design, targets, factor, weights, penalty, solution, residual,
    block, fbuf, ft, tall, direction, dlow,
    psend, precv, p2, p3, pfull,
    vsend, vrecv, v2, v3, vlow,
    load_sem, a_sem, t_sem, p1_sem, p2_sem, p3_sem, v1_sem, v2_sem, v3_sem,
):
    me = lax.axis_index("row")
    mf = lax.axis_index("feat")
    count, rows_dev = targets.shape
    width = block.shape[2]
    rows = n_row * rows_dev
    rank = ft.shape[0]
    part = rank // n_row
    tiles = width // tile
    pending = []

    def send(src, dst, sems, at_dest, at_src, axis, peer):
        copy = pltpu.make_async_remote_copy(
            src_ref=src,
            dst_ref=dst,
            send_sem=sems.at[0, *at_dest],
            recv_sem=sems.at[1, *at_src],
            device_id={axis: peer},
            device_id_type=pl.DeviceIdType.MESH,
        )
        copy.start()
        pending.append(copy)

    def arrived(dst, sems, at_src, axis, peer):
        pltpu.make_async_remote_copy(
            src_ref=dst,
            dst_ref=dst,
            send_sem=sems.at[0, *at_src],
            recv_sem=sems.at[1, *at_src],
            device_id={axis: peer},
            device_id_type=pl.DeviceIdType.MESH,
        ).wait_recv()

    def row_peers():
        return [lax.rem(me + off, n_row) for off in range(1, n_row)]

    def feat_peers():
        return [lax.rem(mf + off, n_feat) for off in range(1, n_feat)]

    load_f = pltpu.make_async_copy(factor, fbuf, load_sem.at[0])
    load_f.start()
    own = pltpu.make_async_copy(
        design.at[:, pl.ds(pl.multiple_of(me * width, width), width)], block.at[me], load_sem.at[1]
    )
    own.start()

    barrier = pltpu.get_barrier_semaphore()
    for peer in row_peers():
        pl.semaphore_signal(
            barrier, inc=1, device_id={"row": peer}, device_id_type=pl.DeviceIdType.MESH
        )
    for peer in feat_peers():
        pl.semaphore_signal(
            barrier, inc=1, device_id={"feat": peer}, device_id_type=pl.DeviceIdType.MESH
        )
    pl.semaphore_wait(barrier, n_row + n_feat - 2)

    my_rows = pl.ds(pl.multiple_of(me * rows_dev, rows_dev), rows_dev)
    for peer in row_peers():
        send(targets, tall.at[:, my_rows], t_sem, (peer,), (me,), "row", peer)
        send(
            design.at[:, pl.ds(pl.multiple_of(peer * width, width), width)],
            block.at[me], a_sem, (peer,), (me,), "row", peer,
        )

    psend[...] = jnp.zeros_like(psend)
    vsend[...] = jnp.zeros_like(vsend)
    for k in range(ITERS):
        p3[k] = jnp.zeros_like(p3[k])
    tall[:, my_rows] = targets[...]
    solution[...] = jnp.zeros_like(solution)
    load_f.wait()
    step_rows = min(width, 256)

    @pl.loop(0, width // step_rows)
    def _(j):
        at = pl.ds(pl.multiple_of(j * step_rows, step_rows), step_rows)
        ft[:, at] = fbuf[at, :].T.astype(BF16)

    own.wait()
    for peer in row_peers():
        arrived(tall.at[:, pl.ds(pl.multiple_of(peer * rows_dev, rows_dev), rows_dev)], t_sem, (peer,), "row", peer)
        arrived(block.at[peer], a_sem, (peer,), "row", peer)

    def times_block(low, at):
        return jnp.dot(low, block[:, :, at].reshape(rows, tile), preferred_element_type=F32)

    @pl.loop(0, tiles)
    def _(j):
        at = pl.ds(pl.multiple_of(j * tile, tile), tile)
        residual[:, at] = times_block(tall[...], at)

    def square_rows(value):
        low = (value * value).astype(BF16)
        sums = lax.dot_general(jnp.ones((EXTRA, width), BF16), low, NT, preferred_element_type=F32)
        at = lax.broadcasted_iota(jnp.int32, sums.shape, 0)
        high = sums.astype(BF16).astype(F32)
        return jnp.where(at == 0, high, jnp.where(at == 1, sums - high, 0.0))

    def row_total(k, sent, received, sems):
        total = sent[k, me].astype(F32)
        for peer in row_peers():
            arrived(received.at[k, peer], sems, (k, peer), "row", peer)
            total = total + received[k, peer].astype(F32)
        return total

    def feat_total(k, total, held, sems):
        held[k, mf] = total
        for peer in feat_peers():
            send(held.at[k, mf], held.at[k, mf], sems, (k, peer), (k, mf), "feat", peer)
        for peer in feat_peers():
            arrived(held.at[k, peer], sems, (k, peer), "feat", peer)
        total = held[k, 0]
        for index in range(1, n_feat):
            total = total + held[k, index]
        return total

    inner = None
    for k in range(ITERS):
        value = residual[...]
        projected = lax.dot_general(ft[...], value.astype(BF16), NT, preferred_element_type=F32)
        squares = square_rows(value).astype(psend.dtype)
        for index in range(n_row):
            psend[k, index, :part, :count] = projected[index * part : (index + 1) * part].astype(
                psend.dtype
            )
            psend[k, index, part:, :count] = squares
        for peer in row_peers():
            send(psend.at[k, peer], precv.at[k, me], p1_sem, (k, peer), (k, me), "row", peer)
        total = feat_total(k, row_total(k, psend, precv, p1_sem), p2, p2_sem)
        norm = jnp.sum(total[part:], axis=0, keepdims=True)
        p3[k] = total[:part].astype(p3.dtype)
        my_part = pl.ds(pl.multiple_of(me * part, part), part)
        pfull[k, my_part, :] = p3[k]
        for peer in row_peers():
            send(p3.at[k], pfull.at[k, my_part, :], p3_sem, (k, peer), (k, me), "row", peer)
        for peer in row_peers():
            arrived(
                pfull.at[k, pl.ds(pl.multiple_of(peer * part, part), part), :],
                p3_sem, (k, peer), "row", peer,
            )
        projected = pfull[k].astype(F32)
        weighted = weights[...] * projected
        inner_next = to_column(norm + jnp.sum(weighted * projected, axis=0, keepdims=True), count)
        weighted_low = weighted.T[:count].astype(BF16)
        ratio = None if inner is None else inner_next / inner
        inner = inner_next

        @pl.loop(0, tiles)
        def _(j):
            at = pl.ds(pl.multiple_of(j * tile, tile), tile)
            search = residual[:, at] + jnp.dot(
                weighted_low, ft[:, at], preferred_element_type=F32
            )
            if ratio is not None:
                search = search + ratio * direction[:, at]
            direction[:, at] = search
            dlow[:, at] = search.astype(BF16)

        squares = square_rows(direction[...]).astype(BF16)
        pairs = n_row // 2
        for off in list(range(1, pairs)) + [0]:
            pair = lax.rem(me // 2 + off, pairs)
            values = lax.dot_general(
                dlow[...],
                block[pl.ds(2 * pair, 2)].reshape(2 * rows_dev, width),
                NT,
                preferred_element_type=F32,
            ).astype(BF16)
            for half in range(2):
                vsend[k, 2 * pair + half, :count, :] = values[
                    :, half * rows_dev : (half + 1) * rows_dev
                ]
                vsend[k, 2 * pair + half, count:, :count] = squares
            if off:
                peers = [2 * pair, 2 * pair + 1]
            else:
                peers = [me + 1 - 2 * lax.rem(me, 2)]
            for peer in peers:
                send(vsend.at[k, peer], vrecv.at[k, me], v1_sem, (k, peer), (k, me), "row", peer)
        total = feat_total(k, row_total(k, vsend, vrecv, v1_sem), v2, v2_sem)
        norm = to_column(jnp.sum(total[count:], axis=0, keepdims=True), count)
        v3[k] = total[:count].astype(BF16)
        vlow[k, :, my_rows] = v3[k]
        for peer in row_peers():
            send(v3.at[k], vlow.at[k, :, my_rows], v3_sem, (k, peer), (k, me), "row", peer)
        for peer in row_peers():
            arrived(
                vlow.at[k, :, pl.ds(pl.multiple_of(peer * rows_dev, rows_dev), rows_dev)],
                v3_sem, (k, peer), "row", peer,
            )
        row_low = vlow[k]
        wide = row_low.astype(F32)
        curvature = jnp.sum(wide * wide, axis=1, keepdims=True) + penalty[...] * norm
        step = inner / curvature
        ridge = penalty[...]

        @pl.loop(0, tiles)
        def _(j):
            at = pl.ds(pl.multiple_of(j * tile, tile), tile)
            along = direction[:, at]
            solution[:, at] = solution[:, at] + step * along
            residual[:, at] = residual[:, at] - step * (times_block(row_low, at) + ridge * along)

    for copy in pending:
        copy.wait_send()


def shards(n_row, n_feat, design, targets, factor, weights, penalty):
    rows_dev, columns = design.shape
    width = columns // n_row
    count = targets.shape[1]
    rank = factor.shape[1]
    rows = n_row * rows_dev
    part = rank // n_row
    link = BF16 if part % 16 == 0 else F32
    vmem = pl.BlockSpec(memory_space=pltpu.VMEM)
    hbm = pl.BlockSpec(memory_space=pl.ANY)
    out = jax.ShapeDtypeStruct((count, width), F32)
    dma = pltpu.SemaphoreType.DMA
    solution, residual = pl.pallas_call(
        functools.partial(kernel, n_row, n_feat, min(width, 512)),
        out_shape=(out, out),
        in_specs=[hbm, vmem, hbm, vmem, vmem],
        out_specs=(vmem, vmem),
        scratch_shapes=[
            pltpu.VMEM((n_row, rows_dev, width), BF16),
            pltpu.VMEM((width, rank), F32),
            pltpu.VMEM((rank, width), BF16),
            pltpu.VMEM((count, rows), BF16),
            pltpu.VMEM((count, width), F32),
            pltpu.VMEM((count, width), BF16),
            pltpu.VMEM((ITERS, n_row, part + EXTRA, LANES), link),
            pltpu.VMEM((ITERS, n_row, part + EXTRA, LANES), link),
            pltpu.VMEM((ITERS, n_feat, part + EXTRA, LANES), F32),
            pltpu.VMEM((ITERS, part, LANES), link),
            pltpu.VMEM((ITERS, rank, LANES), link),
            pltpu.VMEM((ITERS, n_row, count + EXTRA, rows_dev), BF16),
            pltpu.VMEM((ITERS, n_row, count + EXTRA, rows_dev), BF16),
            pltpu.VMEM((ITERS, n_feat, count + EXTRA, rows_dev), F32),
            pltpu.VMEM((ITERS, count, rows_dev), BF16),
            pltpu.VMEM((ITERS, count, rows), BF16),
            dma((2,)),
            dma((2, n_row)),
            dma((2, n_row)),
            dma((2, ITERS, n_row)),
            dma((2, ITERS, n_feat)),
            dma((2, ITERS, n_row)),
            dma((2, ITERS, n_row)),
            dma((2, ITERS, n_feat)),
            dma((2, ITERS, n_row)),
        ],
        compiler_params=pltpu.CompilerParams(
            collective_id=0, has_side_effects=True, vmem_limit_bytes=40 * 1024 * 1024
        ),
    )(design, targets.T, factor, weights[:, None], penalty[:, None])
    return solution.T, residual.T


def solution(mesh):
    return jax.shard_map(
        functools.partial(shards, mesh.shape["row"], mesh.shape["feat"]),
        mesh=mesh,
        in_specs=(P("row", "feat"), P("row", None), P(("feat", "row"), None), P(), P()),
        out_specs=(P(("feat", "row"), None), P(("feat", "row"), None)),
        check_vma=False,
    )
```

```python
import functools

import jax
import jax.numpy as jnp
from jax import lax
from jax.experimental import pallas as pl
from jax.experimental.pallas import tpu as pltpu
from jax.sharding import PartitionSpec as P

ITERS = 3
EXTRA = 16
LANES = 128
F32 = jnp.float32
BF16 = jnp.bfloat16
NT = (((1,), (1,)), ((), ()))


def to_column(row, count):
    return jnp.broadcast_to(row, (LANES, LANES)).T[:count, :1]


def kernel(
    n_row, n_feat, tile,
    design, targets, factor, weights, penalty, solution, residual,
    block, fbuf, ft, tlocal, wrow, prow, tall, direction, dlow,
    psend, precv, p2, p3, pfull,
    vsend, vrecv, v2, v3, vlow,
    load_sem, a_sem, t_sem, p1_sem, p2_sem, p3_sem, v1_sem, v2_sem, v3_sem,
):
    me = lax.axis_index("row")
    mf = lax.axis_index("feat")
    count, rows_dev = tlocal.shape
    width = block.shape[2]
    rows = n_row * rows_dev
    rank = ft.shape[0]
    part = rank // n_row
    tiles = width // tile
    pending = []

    def send(src, dst, sems, at_dest, at_src, axis, peer):
        copy = pltpu.make_async_remote_copy(
            src_ref=src,
            dst_ref=dst,
            send_sem=sems.at[0, *at_dest],
            recv_sem=sems.at[1, *at_src],
            device_id={axis: peer},
            device_id_type=pl.DeviceIdType.MESH,
        )
        copy.start()
        pending.append(copy)

    def arrived(dst, sems, at_src, axis, peer):
        pltpu.make_async_remote_copy(
            src_ref=dst,
            dst_ref=dst,
            send_sem=sems.at[0, *at_src],
            recv_sem=sems.at[1, *at_src],
            device_id={axis: peer},
            device_id_type=pl.DeviceIdType.MESH,
        ).wait_recv()

    def row_peers():
        return [lax.rem(me + off, n_row) for off in range(1, n_row)]

    def feat_peers():
        return [lax.rem(mf + off, n_feat) for off in range(1, n_feat)]

    load_t = pltpu.make_async_copy(targets, tlocal, load_sem.at[2])
    load_t.start()
    load_w = pltpu.make_async_copy(weights, wrow, load_sem.at[3])
    load_w.start()
    load_p = pltpu.make_async_copy(penalty, prow, load_sem.at[4])
    load_p.start()
    load_f = pltpu.make_async_copy(factor, fbuf, load_sem.at[0])
    load_f.start()
    own = pltpu.make_async_copy(
        design.at[:, pl.ds(pl.multiple_of(me * width, width), width)], block.at[me], load_sem.at[1]
    )
    own.start()

    barrier = pltpu.get_barrier_semaphore()
    for peer in row_peers():
        pl.semaphore_signal(
            barrier, inc=1, device_id={"row": peer}, device_id_type=pl.DeviceIdType.MESH
        )
    for peer in feat_peers():
        pl.semaphore_signal(
            barrier, inc=1, device_id={"feat": peer}, device_id_type=pl.DeviceIdType.MESH
        )
    pl.semaphore_wait(barrier, n_row + n_feat - 2)

    my_rows = pl.ds(pl.multiple_of(me * rows_dev, rows_dev), rows_dev)
    load_t.wait()
    for peer in row_peers():
        send(tlocal, tall.at[:, my_rows], t_sem, (peer,), (me,), "row", peer)
        send(
            design.at[:, pl.ds(pl.multiple_of(peer * width, width), width)],
            block.at[me], a_sem, (peer,), (me,), "row", peer,
        )

    psend[...] = jnp.zeros_like(psend)
    vsend[...] = jnp.zeros_like(vsend)
    for k in range(ITERS):
        p3[k] = jnp.zeros_like(p3[k])
    tall[:, my_rows] = tlocal[...]
    solution[...] = jnp.zeros_like(solution)
    load_f.wait()
    step_rows = min(width, 256)

    @pl.loop(0, width // step_rows)
    def _(j):
        at = pl.ds(pl.multiple_of(j * step_rows, step_rows), step_rows)
        ft[:, at] = fbuf[at, :].T.astype(BF16)

    load_w.wait()
    load_p.wait()
    weight = jnp.broadcast_to(wrow[...], (LANES, rank)).T[:, :1]
    ridge = jnp.broadcast_to(prow[...], (LANES, LANES)).T[:count, :1]
    own.wait()

    def first_product(source, fresh):
        low = tall[:, pl.ds(pl.multiple_of(source * rows_dev, rows_dev), rows_dev)]

        @pl.loop(0, tiles)
        def _(j):
            at = pl.ds(pl.multiple_of(j * tile, tile), tile)
            value = jnp.dot(low, block[source, :, at], preferred_element_type=F32)
            residual[:, at] = value if fresh else residual[:, at] + value

    first_product(me, True)
    for off in range(1, n_row):
        peer = lax.rem(me + n_row - off, n_row)
        arrived(tall.at[:, pl.ds(pl.multiple_of(peer * rows_dev, rows_dev), rows_dev)], t_sem, (peer,), "row", peer)
        arrived(block.at[peer], a_sem, (peer,), "row", peer)
        first_product(peer, False)

    def times_block(low, at):
        return jnp.dot(low, block[:, :, at].reshape(rows, tile), preferred_element_type=F32)

    def square_rows(value):
        low = (value * value).astype(BF16)
        sums = lax.dot_general(jnp.ones((EXTRA, width), BF16), low, NT, preferred_element_type=F32)
        at = lax.broadcasted_iota(jnp.int32, sums.shape, 0)
        high = sums.astype(BF16).astype(F32)
        return jnp.where(at == 0, high, jnp.where(at == 1, sums - high, 0.0))

    def row_total(k, sent, received, sems):
        total = sent[k, me].astype(F32)
        for peer in row_peers():
            arrived(received.at[k, peer], sems, (k, peer), "row", peer)
            total = total + received[k, peer].astype(F32)
        return total

    def feat_total(k, total, held, sems):
        held[k, mf] = total
        for peer in feat_peers():
            send(held.at[k, mf], held.at[k, mf], sems, (k, peer), (k, mf), "feat", peer)
        for peer in feat_peers():
            arrived(held.at[k, peer], sems, (k, peer), "feat", peer)
        total = held[k, 0]
        for index in range(1, n_feat):
            total = total + held[k, index]
        return total

    inner = None
    for k in range(ITERS):
        value = residual[...]
        projected = lax.dot_general(ft[...], value.astype(BF16), NT, preferred_element_type=F32)
        squares = square_rows(value).astype(psend.dtype)
        for index in range(n_row):
            psend[k, index, :part, :count] = projected[index * part : (index + 1) * part].astype(
                psend.dtype
            )
            psend[k, index, part:, :count] = squares
        for peer in row_peers():
            send(psend.at[k, peer], precv.at[k, me], p1_sem, (k, peer), (k, me), "row", peer)
        total = feat_total(k, row_total(k, psend, precv, p1_sem), p2, p2_sem)
        norm = jnp.sum(total[part:], axis=0, keepdims=True)
        p3[k] = total[:part].astype(p3.dtype)
        my_part = pl.ds(pl.multiple_of(me * part, part), part)
        pfull[k, my_part, :] = p3[k]
        for peer in row_peers():
            send(p3.at[k], pfull.at[k, my_part, :], p3_sem, (k, peer), (k, me), "row", peer)
        for peer in row_peers():
            arrived(
                pfull.at[k, pl.ds(pl.multiple_of(peer * part, part), part), :],
                p3_sem, (k, peer), "row", peer,
            )
        projected = pfull[k].astype(F32)
        weighted = weight * projected
        inner_next = to_column(norm + jnp.sum(weighted * projected, axis=0, keepdims=True), count)
        weighted_low = weighted.T[:count].astype(BF16)
        ratio = None if inner is None else inner_next / inner
        inner = inner_next

        @pl.loop(0, tiles)
        def _(j):
            at = pl.ds(pl.multiple_of(j * tile, tile), tile)
            search = residual[:, at] + jnp.dot(
                weighted_low, ft[:, at], preferred_element_type=F32
            )
            if ratio is not None:
                search = search + ratio * direction[:, at]
            direction[:, at] = search
            dlow[:, at] = search.astype(BF16)

        squares = square_rows(direction[...]).astype(BF16)
        pairs = n_row // 2
        for off in list(range(1, pairs)) + [0]:
            pair = lax.rem(me // 2 + off, pairs)
            values = lax.dot_general(
                dlow[...],
                block[pl.ds(2 * pair, 2)].reshape(2 * rows_dev, width),
                NT,
                preferred_element_type=F32,
            ).astype(BF16)
            for half in range(2):
                vsend[k, 2 * pair + half, :count, :] = values[
                    :, half * rows_dev : (half + 1) * rows_dev
                ]
                vsend[k, 2 * pair + half, count:, :count] = squares
            if off:
                peers = [2 * pair, 2 * pair + 1]
            else:
                peers = [me + 1 - 2 * lax.rem(me, 2)]
            for peer in peers:
                send(vsend.at[k, peer], vrecv.at[k, me], v1_sem, (k, peer), (k, me), "row", peer)
        total = feat_total(k, row_total(k, vsend, vrecv, v1_sem), v2, v2_sem)
        norm = to_column(jnp.sum(total[count:], axis=0, keepdims=True), count)
        v3[k] = total[:count].astype(BF16)
        vlow[k, :, my_rows] = v3[k]
        for peer in row_peers():
            send(v3.at[k], vlow.at[k, :, my_rows], v3_sem, (k, peer), (k, me), "row", peer)
        for peer in row_peers():
            arrived(
                vlow.at[k, :, pl.ds(pl.multiple_of(peer * rows_dev, rows_dev), rows_dev)],
                v3_sem, (k, peer), "row", peer,
            )
        row_low = vlow[k]
        wide = row_low.astype(F32)
        curvature = jnp.sum(wide * wide, axis=1, keepdims=True) + ridge * norm
        step = inner / curvature

        @pl.loop(0, tiles)
        def _(j):
            at = pl.ds(pl.multiple_of(j * tile, tile), tile)
            along = direction[:, at]
            solution[:, at] = solution[:, at] + step * along
            residual[:, at] = residual[:, at] - step * (times_block(row_low, at) + ridge * along)

    for copy in pending:
        copy.wait_send()


def shards(n_row, n_feat, design, targets, factor, weights, penalty):
    rows_dev, columns = design.shape
    width = columns // n_row
    count = targets.shape[1]
    rank = factor.shape[1]
    rows = n_row * rows_dev
    part = rank // n_row
    link = BF16 if part % 16 == 0 else F32
    vmem = pl.BlockSpec(memory_space=pltpu.VMEM)
    hbm = pl.BlockSpec(memory_space=pltpu.HBM)
    out = jax.ShapeDtypeStruct((count, width), F32)
    dma = pltpu.SemaphoreType.DMA
    solution, residual = pl.pallas_call(
        functools.partial(kernel, n_row, n_feat, min(width, 512)),
        out_shape=(out, out),
        in_specs=[hbm] * 5,
        out_specs=(vmem, vmem),
        scratch_shapes=[
            pltpu.VMEM((n_row, rows_dev, width), BF16),
            pltpu.VMEM((width, rank), F32),
            pltpu.VMEM((rank, width), BF16),
            pltpu.VMEM((count, rows_dev), BF16),
            pltpu.VMEM((1, rank), F32),
            pltpu.VMEM((1, LANES), F32),
            pltpu.VMEM((count, rows), BF16),
            pltpu.VMEM((count, width), F32),
            pltpu.VMEM((count, width), BF16),
            pltpu.VMEM((ITERS, n_row, part + EXTRA, LANES), link),
            pltpu.VMEM((ITERS, n_row, part + EXTRA, LANES), link),
            pltpu.VMEM((ITERS, n_feat, part + EXTRA, LANES), F32),
            pltpu.VMEM((ITERS, part, LANES), link),
            pltpu.VMEM((ITERS, rank, LANES), link),
            pltpu.VMEM((ITERS, n_row, count + EXTRA, rows_dev), BF16),
            pltpu.VMEM((ITERS, n_row, count + EXTRA, rows_dev), BF16),
            pltpu.VMEM((ITERS, n_feat, count + EXTRA, rows_dev), F32),
            pltpu.VMEM((ITERS, count, rows_dev), BF16),
            pltpu.VMEM((ITERS, count, rows), BF16),
            dma((5,)),
            dma((2, n_row)),
            dma((2, n_row)),
            dma((2, ITERS, n_row)),
            dma((2, ITERS, n_feat)),
            dma((2, ITERS, n_row)),
            dma((2, ITERS, n_row)),
            dma((2, ITERS, n_feat)),
            dma((2, ITERS, n_row)),
        ],
        compiler_params=pltpu.CompilerParams(
            collective_id=0, has_side_effects=True, vmem_limit_bytes=65_000_000
        ),
    )(design, targets.T, factor, weights[None, :], jnp.pad(penalty, (0, LANES - count))[None, :])
    return solution.T, residual.T


def solution(mesh):
    return jax.shard_map(
        functools.partial(shards, mesh.shape["row"], mesh.shape["feat"]),
        mesh=mesh,
        in_specs=(P("row", "feat"), P("row", None), P(("feat", "row"), None), P(), P()),
        out_specs=(P(("feat", "row"), None), P(("feat", "row"), None)),
        check_vma=False,
    )
```

```python
import functools

import jax
import jax.numpy as jnp
from jax import lax
from jax.experimental import pallas as pl
from jax.experimental.pallas import tpu as pltpu
from jax.sharding import PartitionSpec as P

ITERS = 3
EXTRA = 16
LANES = 128
F32 = jnp.float32
BF16 = jnp.bfloat16
NT = (((1,), (1,)), ((), ()))


def to_column(row, count):
    return jnp.broadcast_to(row, (LANES, LANES)).T[:count, :1]


def kernel(
    n_row, n_feat, tile,
    design, targets, factor, weights, penalty, solution, residual,
    block, fbuf, ft, tlocal, wrow, prow, tall, direction, dlow,
    psend, precv, p2, p3, pfull,
    vsend, vrecv, v2, v3, vlow,
    kown, csend, crecv, cmid, crow, cfull,
    msend, mrecv, m2, m3, mfull,
    load_sem, a_sem, t_sem, p1_sem, p2_sem, p3_sem, v1_sem, v2_sem, v3_sem,
    ca_sem, cb_sem, cc_sem, cd_sem, m1_sem, m2_sem, m3_sem,
):
    me = lax.axis_index("row")
    mf = lax.axis_index("feat")
    count, rows_dev = tlocal.shape
    width = block.shape[2]
    rows = n_row * rows_dev
    rank = ft.shape[0]
    part = rank // n_row
    tiles = width // tile
    piece = rows_dev // n_feat
    pending = []

    def send(src, dst, sems, at_dest, at_src, axis, peer):
        copy = pltpu.make_async_remote_copy(
            src_ref=src,
            dst_ref=dst,
            send_sem=sems.at[0, *at_dest],
            recv_sem=sems.at[1, *at_src],
            device_id={axis: peer},
            device_id_type=pl.DeviceIdType.MESH,
        )
        copy.start()
        pending.append(copy)

    def arrived(dst, sems, at_src, axis, peer):
        pltpu.make_async_remote_copy(
            src_ref=dst,
            dst_ref=dst,
            send_sem=sems.at[0, *at_src],
            recv_sem=sems.at[1, *at_src],
            device_id={axis: peer},
            device_id_type=pl.DeviceIdType.MESH,
        ).wait_recv()

    def row_peers():
        return [lax.rem(me + off, n_row) for off in range(1, n_row)]

    def feat_peers():
        return [lax.rem(mf + off, n_feat) for off in range(1, n_feat)]

    load_t = pltpu.make_async_copy(targets, tlocal, load_sem.at[2])
    load_t.start()
    load_w = pltpu.make_async_copy(weights, wrow, load_sem.at[3])
    load_w.start()
    load_p = pltpu.make_async_copy(penalty, prow, load_sem.at[4])
    load_p.start()
    load_f = pltpu.make_async_copy(factor, fbuf, load_sem.at[0])
    load_f.start()
    own = pltpu.make_async_copy(
        design.at[:, pl.ds(pl.multiple_of(me * width, width), width)], block.at[me], load_sem.at[1]
    )
    own.start()

    barrier = pltpu.get_barrier_semaphore()
    for peer in row_peers():
        pl.semaphore_signal(
            barrier, inc=1, device_id={"row": peer}, device_id_type=pl.DeviceIdType.MESH
        )
    for peer in feat_peers():
        pl.semaphore_signal(
            barrier, inc=1, device_id={"feat": peer}, device_id_type=pl.DeviceIdType.MESH
        )
    pl.semaphore_wait(barrier, n_row + n_feat - 2)

    my_rows = pl.ds(pl.multiple_of(me * rows_dev, rows_dev), rows_dev)
    load_t.wait()
    for peer in row_peers():
        send(tlocal, tall.at[:, my_rows], t_sem, (peer,), (me,), "row", peer)
        send(
            design.at[:, pl.ds(pl.multiple_of(peer * width, width), width)],
            block.at[me], a_sem, (peer,), (me,), "row", peer,
        )

    psend[...] = jnp.zeros_like(psend)
    vsend[...] = jnp.zeros_like(vsend)
    msend[...] = jnp.zeros_like(msend)
    p3[...] = jnp.zeros_like(p3)
    tall[:, my_rows] = tlocal[...]
    solution[...] = jnp.zeros_like(solution)
    load_f.wait()
    step_rows = min(width, 256)

    @pl.loop(0, width // step_rows)
    def _(j):
        at = pl.ds(pl.multiple_of(j * step_rows, step_rows), step_rows)
        ft[:, at] = fbuf[at, :].T.astype(BF16)

    kown[...] = lax.dot_general(ft[...], ft[...], NT, preferred_element_type=F32)
    load_w.wait()
    load_p.wait()
    weight = jnp.broadcast_to(wrow[...], (LANES, rank)).T[:, :1]
    ridge = jnp.broadcast_to(prow[...], (LANES, LANES)).T[:count, :1]
    own.wait()

    def first_product(source, fresh):
        low = tall[:, pl.ds(pl.multiple_of(source * rows_dev, rows_dev), rows_dev)]

        @pl.loop(0, tiles)
        def _(j):
            at = pl.ds(pl.multiple_of(j * tile, tile), tile)
            value = jnp.dot(low, block[source, :, at], preferred_element_type=F32)
            residual[:, at] = value if fresh else residual[:, at] + value

    def cross_product(source):
        cross = lax.dot_general(block[source], ft[...], NT, preferred_element_type=F32).astype(BF16)
        for index in range(n_feat):
            csend[source, index, :piece] = cross[index * piece : (index + 1) * piece]
            at = lax.rem(source * n_feat + index, rank // EXTRA) * EXTRA
            csend[source, index, piece:] = kown[pl.ds(pl.multiple_of(at, EXTRA), EXTRA), :].astype(
                BF16
            )
        for peer in feat_peers():
            send(
                csend.at[source, peer], crecv.at[source, mf],
                ca_sem, (source, peer), (source, mf), "feat", peer,
            )

    first_product(me, True)
    cross_product(me)
    for off in range(1, n_row):
        peer = lax.rem(me + n_row - off, n_row)
        arrived(tall.at[:, pl.ds(pl.multiple_of(peer * rows_dev, rows_dev), rows_dev)], t_sem, (peer,), "row", peer)
        arrived(block.at[peer], a_sem, (peer,), "row", peer)
        first_product(peer, False)
        cross_product(peer)

    def times_block(low, at):
        return jnp.dot(low, block[:, :, at].reshape(rows, tile), preferred_element_type=F32)

    def product_rows(left, right, first):
        low = (left * right).astype(BF16)
        sums = lax.dot_general(jnp.ones((EXTRA, width), BF16), low, NT, preferred_element_type=F32)
        at = lax.broadcasted_iota(jnp.int32, sums.shape, 0)
        high = sums.astype(BF16).astype(F32)
        return jnp.where(at == first, high, jnp.where(at == first + 1, sums - high, 0.0))

    def square_rows(value):
        return product_rows(value, value, 0)

    def cross_to_rows():
        for index in range(n_row):
            for peer in feat_peers():
                arrived(crecv.at[index, peer], ca_sem, (index, peer), "feat", peer)
        for index in range(n_row):
            total = csend[index, mf].astype(F32)
            for off in range(1, n_feat):
                total = total + crecv[index, lax.rem(mf + off, n_feat)].astype(F32)
            cmid[index] = total.astype(BF16)
        for peer in row_peers():
            send(cmid.at[peer], crow.at[me], cb_sem, (peer,), (me,), "row", peer)

    def cross_gather():
        total = cmid[me].astype(F32)
        for peer in row_peers():
            arrived(crow.at[peer], cb_sem, (peer,), "row", peer)
            total = total + crow[peer].astype(F32)
        cfull[me, mf] = total.astype(BF16)
        for peer in row_peers():
            send(cfull.at[me, mf], cfull.at[me, mf], cc_sem, (peer,), (me,), "row", peer)

    def cross_spread():
        for peer in row_peers():
            arrived(cfull.at[peer, mf], cc_sem, (peer,), "row", peer)
        for peer in feat_peers():
            send(cfull.at[:, mf], cfull.at[:, mf], cd_sem, (peer,), (mf,), "feat", peer)

    def cross_finish():
        for peer in feat_peers():
            arrived(cfull.at[:, peer], cd_sem, (peer,), "feat", peer)
        used = rank // EXTRA // n_feat
        return (
            cfull[:, :, :piece, :].reshape(rows, rank),
            cfull[:used, :, piece:, :].reshape(rank, rank),
        )

    def send_products(k, low, sent, received, sems):
        pairs = n_row // 2
        for off in list(range(1, pairs)) + [0]:
            pair = lax.rem(me // 2 + off, pairs)
            values = lax.dot_general(
                low,
                block[pl.ds(2 * pair, 2)].reshape(2 * rows_dev, width),
                NT,
                preferred_element_type=F32,
            ).astype(BF16)
            for half in range(2):
                sent[k, 2 * pair + half, :count, :] = values[
                    :, half * rows_dev : (half + 1) * rows_dev
                ]
            if off:
                peers = [2 * pair, 2 * pair + 1]
            else:
                peers = [me + 1 - 2 * lax.rem(me, 2)]
            for peer in peers:
                send(sent.at[k, peer], received.at[k, me], sems, (k, peer), (k, me), "row", peer)

    def row_total(k, sent, received, sems):
        total = sent[k, me].astype(F32)
        for peer in row_peers():
            arrived(received.at[k, peer], sems, (k, peer), "row", peer)
            total = total + received[k, peer].astype(F32)
        return total

    def feat_total(k, total, held, sems):
        held[k, mf] = total
        for peer in feat_peers():
            send(held.at[k, mf], held.at[k, mf], sems, (k, peer), (k, mf), "feat", peer)
        for peer in feat_peers():
            arrived(held.at[k, peer], sems, (k, peer), "feat", peer)
        total = held[k, 0]
        for index in range(1, n_feat):
            total = total + held[k, index]
        return total

    for k in range(1):
        value = residual[...]
        projected = lax.dot_general(ft[...], value.astype(BF16), NT, preferred_element_type=F32)
        squares = square_rows(value).astype(psend.dtype)
        for index in range(n_row):
            psend[k, index, :part, :count] = projected[index * part : (index + 1) * part].astype(
                psend.dtype
            )
            psend[k, index, part:, :count] = squares
        for peer in row_peers():
            send(psend.at[k, peer], precv.at[k, me], p1_sem, (k, peer), (k, me), "row", peer)
        cross_to_rows()
        total = feat_total(k, row_total(k, psend, precv, p1_sem), p2, p2_sem)
        norm = jnp.sum(total[part:], axis=0, keepdims=True)
        p3[k] = total[:part].astype(p3.dtype)
        my_part = pl.ds(pl.multiple_of(me * part, part), part)
        pfull[k, my_part, :] = p3[k]
        for peer in row_peers():
            send(p3.at[k], pfull.at[k, my_part, :], p3_sem, (k, peer), (k, me), "row", peer)
        for peer in row_peers():
            arrived(
                pfull.at[k, pl.ds(pl.multiple_of(peer * part, part), part), :],
                p3_sem, (k, peer), "row", peer,
            )
        projected = pfull[k].astype(F32)
        weighted = weight * projected
        inner_row = norm + jnp.sum(weighted * projected, axis=0, keepdims=True)
        inner = to_column(inner_row, count)
        weighted_low = weighted.T[:count].astype(BF16)

        @pl.loop(0, tiles)
        def _(j):
            at = pl.ds(pl.multiple_of(j * tile, tile), tile)
            search = residual[:, at] + jnp.dot(
                weighted_low, ft[:, at], preferred_element_type=F32
            )
            direction[:, at] = search
            dlow[:, at] = search.astype(BF16)

        squares = square_rows(direction[...]).astype(BF16)
        for index in range(n_row):
            vsend[k, index, count:, :count] = squares
        send_products(k, dlow[...], vsend, vrecv, v1_sem)
        cross_gather()
        total = feat_total(k, row_total(k, vsend, vrecv, v1_sem), v2, v2_sem)
        norm_row = jnp.sum(total[count:], axis=0, keepdims=True)
        norm = to_column(norm_row, count)
        v3[k] = total[:count].astype(BF16)
        vlow[k, :, my_rows] = v3[k]
        for peer in row_peers():
            send(v3.at[k], vlow.at[k, :, my_rows], v3_sem, (k, peer), (k, me), "row", peer)
        cross_spread()
        for peer in row_peers():
            arrived(
                vlow.at[k, :, pl.ds(pl.multiple_of(peer * rows_dev, rows_dev), rows_dev)],
                v3_sem, (k, peer), "row", peer,
            )
        row_low = vlow[k]
        wide = row_low.astype(F32)
        curvature = jnp.sum(wide * wide, axis=1, keepdims=True) + ridge * norm
        step = inner / curvature

        @pl.loop(0, tiles)
        def _(j):
            at = pl.ds(pl.multiple_of(j * tile, tile), tile)
            along = direction[:, at]
            solution[:, at] = solution[:, at] + step * along
            residual[:, at] = residual[:, at] - step * (times_block(row_low, at) + ridge * along)

    low_cross = low_gram = None
    previous = wide
    for k in range(ITERS - 1):
        value = residual[...]
        dlow[...] = value.astype(BF16)
        raw = lax.dot_general(ft[...], dlow[...], NT, preferred_element_type=F32).astype(BF16)
        stats = (
            product_rows(value, value, 0) + product_rows(direction[...], value, 2)
        ).astype(BF16)
        for index in range(n_row):
            msend[k, index, count : count + part, :count] = raw[index * part : (index + 1) * part]
            msend[k, index, count + part :, :count] = stats
        send_products(k, dlow[...], msend, mrecv, m1_sem)
        total = feat_total(k, row_total(k, msend, mrecv, m1_sem), m2, m2_sem)
        m3[k] = total[: count + part].astype(BF16)
        mfull[k, me] = m3[k]
        for peer in row_peers():
            send(m3.at[k], mfull.at[k, me], m3_sem, (k, peer), (k, me), "row", peer)
        if low_cross is None:
            low_cross, low_gram = cross_finish()
            along_gram = jnp.dot(low_gram, weighted.astype(BF16), preferred_element_type=F32)
            along = projected + along_gram
        tail = total[count + part :]
        at = lax.broadcasted_iota(jnp.int32, tail.shape, 0)
        norm = jnp.sum(jnp.where(at < 2, tail, 0.0), axis=0, keepdims=True)
        overlap = jnp.sum(jnp.where(at >= 2, tail, 0.0), axis=0, keepdims=True)
        for peer in row_peers():
            arrived(mfull.at[k, peer], m3_sem, (k, peer), "row", peer)
        image = jnp.concatenate([mfull[k, q, :count, :] for q in range(n_row)], axis=1).astype(F32)
        projected = jnp.concatenate(
            [mfull[k, q, count:, :].astype(F32) for q in range(n_row)], axis=0
        )
        weighted = weight * projected
        weighted_low = weighted.T[:count].astype(BF16)
        gain = jnp.sum(weighted * projected, axis=0, keepdims=True)
        ratio_row = (norm + gain) / inner_row
        inner_row = norm + gain
        inner = to_column(inner_row, count)
        ratio = to_column(ratio_row, count)
        image = image + lax.dot_general(weighted_low, low_cross, NT, preferred_element_type=F32)
        image = image + ratio * previous
        row_low = image.astype(BF16)
        wide = row_low.astype(F32)
        previous = image
        along_gram = jnp.dot(low_gram, weighted.astype(BF16), preferred_element_type=F32)
        squared = norm + 2.0 * gain + jnp.sum(weighted * along_gram, axis=0, keepdims=True)
        mixed = overlap + jnp.sum(along * weighted, axis=0, keepdims=True)
        norm_row = squared + 2.0 * ratio_row * mixed + ratio_row * ratio_row * norm_row
        along = projected + along_gram + ratio_row * along
        curvature = jnp.sum(wide * wide, axis=1, keepdims=True) + ridge * to_column(norm_row, count)
        step = inner / curvature

        @pl.loop(0, tiles)
        def _(j):
            at = pl.ds(pl.multiple_of(j * tile, tile), tile)
            search = residual[:, at] + jnp.dot(
                weighted_low, ft[:, at], preferred_element_type=F32
            )
            search = search + ratio * direction[:, at]
            direction[:, at] = search
            solution[:, at] = solution[:, at] + step * search
            residual[:, at] = residual[:, at] - step * (times_block(row_low, at) + ridge * search)

    for copy in pending:
        copy.wait_send()


def shards(n_row, n_feat, design, targets, factor, weights, penalty):
    rows_dev, columns = design.shape
    width = columns // n_row
    count = targets.shape[1]
    rank = factor.shape[1]
    rows = n_row * rows_dev
    part = rank // n_row
    piece = rows_dev // n_feat + EXTRA
    merged = count + part + EXTRA
    link = BF16 if part % 16 == 0 else F32
    vmem = pl.BlockSpec(memory_space=pltpu.VMEM)
    hbm = pl.BlockSpec(memory_space=pltpu.HBM)
    out = jax.ShapeDtypeStruct((count, width), F32)
    dma = pltpu.SemaphoreType.DMA
    solution, residual = pl.pallas_call(
        functools.partial(kernel, n_row, n_feat, min(width, 512)),
        out_shape=(out, out),
        in_specs=[hbm] * 5,
        out_specs=(vmem, vmem),
        scratch_shapes=[
            pltpu.VMEM((n_row, rows_dev, width), BF16),
            pltpu.VMEM((width, rank), F32),
            pltpu.VMEM((rank, width), BF16),
            pltpu.VMEM((count, rows_dev), BF16),
            pltpu.VMEM((1, rank), F32),
            pltpu.VMEM((1, LANES), F32),
            pltpu.VMEM((count, rows), BF16),
            pltpu.VMEM((count, width), F32),
            pltpu.VMEM((count, width), BF16),
            pltpu.VMEM((1, n_row, part + EXTRA, LANES), link),
            pltpu.VMEM((1, n_row, part + EXTRA, LANES), link),
            pltpu.VMEM((1, n_feat, part + EXTRA, LANES), F32),
            pltpu.VMEM((1, part, LANES), link),
            pltpu.VMEM((1, rank, LANES), link),
            pltpu.VMEM((1, n_row, count + EXTRA, rows_dev), BF16),
            pltpu.VMEM((1, n_row, count + EXTRA, rows_dev), BF16),
            pltpu.VMEM((1, n_feat, count + EXTRA, rows_dev), F32),
            pltpu.VMEM((1, count, rows_dev), BF16),
            pltpu.VMEM((1, count, rows), BF16),
            pltpu.VMEM((rank, rank), F32),
            pltpu.VMEM((n_row, n_feat, piece, rank), BF16),
            pltpu.VMEM((n_row, n_feat, piece, rank), BF16),
            pltpu.VMEM((n_row, piece, rank), BF16),
            pltpu.VMEM((n_row, piece, rank), BF16),
            pltpu.VMEM((n_row, n_feat, piece, rank), BF16),
            pltpu.VMEM((ITERS - 1, n_row, merged, rows_dev), BF16),
            pltpu.VMEM((ITERS - 1, n_row, merged, rows_dev), BF16),
            pltpu.VMEM((ITERS - 1, n_feat, merged, rows_dev), F32),
            pltpu.VMEM((ITERS - 1, count + part, rows_dev), BF16),
            pltpu.VMEM((ITERS - 1, n_row, count + part, rows_dev), BF16),
            dma((5,)),
            dma((2, n_row)),
            dma((2, n_row)),
            dma((2, 1, n_row)),
            dma((2, 1, n_feat)),
            dma((2, 1, n_row)),
            dma((2, 1, n_row)),
            dma((2, 1, n_feat)),
            dma((2, 1, n_row)),
            dma((2, n_row, n_feat)),
            dma((2, n_row)),
            dma((2, n_row)),
            dma((2, n_feat)),
            dma((2, ITERS - 1, n_row)),
            dma((2, ITERS - 1, n_feat)),
            dma((2, ITERS - 1, n_row)),
        ],
        compiler_params=pltpu.CompilerParams(
            collective_id=0, has_side_effects=True, vmem_limit_bytes=65_000_000
        ),
    )(design, targets.T, factor, weights[None, :], jnp.pad(penalty, (0, LANES - count))[None, :])
    return solution.T, residual.T


def solution(mesh):
    return jax.shard_map(
        functools.partial(shards, mesh.shape["row"], mesh.shape["feat"]),
        mesh=mesh,
        in_specs=(P("row", "feat"), P("row", None), P(("feat", "row"), None), P(), P()),
        out_specs=(P(("feat", "row"), None), P(("feat", "row"), None)),
        check_vma=False,
    )
```
